32 devices in a mesh: row: 4 (over z), col: 4 (over y, x), wave: 2 (over core).
Axes of the slice: x: 2, y: 2, z: 4, core: 2. Of those that a mesh axis runs over, the one named last changes fastest.
Arguments:
- transmission: float32 [4096, 4096], P('row', 'col'), may hold values from 0 to 1
- dual_focal: float32 [512, 8, 512], P(('row', 'col'), 'wave'), may hold values from -12 to 12
- dual_curvature: float32 [4096, 4096], P('row', 'col'), may hold values from -6 to 6
- pupil_mask: int32 [4096, 4096], P('row', 'col'), may hold values 0 or 1
- lyot_mask: int32 [4096, 4096], P('row', 'col'), may hold values 0 or 1
- dark_mask: int32 [512, 8, 512], P(('row', 'col'), 'wave'), may hold values 0 or 1
- focal_rows: float32 [8, 512, 4096], P('wave', None, 'row'), may hold values from -0.09375 to 0.09375
- focal_cols: float32 [8, 512, 4096], P('wave', None, 'col'), may hold values from -0.09375 to 0.09375
Outputs:
- transmission_out: float32 [4096, 4096], P('row', 'col')
- dual_focal_out: float32 [512, 8, 512], P(('row', 'col'), 'wave')
- dual_curvature_out: float32 [4096, 4096], P('row', 'col')
The draws below stay inside these ranges and needn't reach their ends.
All inputs are finite; a program needn't handle non-finite values. No bound on the sum of `pupil_mask` or of `lyot_mask` or of `dark_mask` on one device may be relied on, other than what follows from the above.
Results may differ from the reference program's by a relative error of at most 0.0001.
Values sent between devices are 32-bit elements; how exact they have to be, the bound alone decides.
A program may use at most 128 MiB of HBM per device.

```python
import jax
import jax.numpy as jnp
from jax import lax

N = 4096
Z = 512
NW = 8
ITERS = 2


def with_ends(drawn, stream_key, smallest, high):
    longest = drawn.shape.index(max(drawn.shape))
    spots = []
    for shift in (0, 1):
        where = [jax.random.randint(jax.random.fold_in(stream_key, axis), (), 0, length) for axis, length in enumerate(drawn.shape)]
        where[longest] = (where[longest] + shift) % drawn.shape[longest]
        spots.append(tuple(where))
    return drawn.at[spots[0]].set(smallest).at[spots[1]].set(high)


def steps_of(rng, extent, shards, smallest, high):
    loudness, own = 1.0, jax.random.fold_in(rng, 6)
    for dim, parts in shards:
        steps = jnp.exp(jax.random.uniform(jax.random.fold_in(own, dim), (parts,), jnp.float32, smallest / len(shards), high / len(shards)))
        loudness = loudness * jnp.repeat(steps, extent[dim] // parts).reshape([-1 if axis == dim else 1 for axis in range(len(extent))])
    return loudness


def centred(stream_key, dims, scale, most, pieces=(), held_as=jnp.bfloat16):
    drawn = jax.random.normal(stream_key, dims, jnp.float32) * scale
    if len(pieces) > 0:
        drawn = steps_of(stream_key, dims, pieces, -0.22, 0.18) * drawn
    return jnp.clip(drawn, min=-most, max=most).astype(held_as)


def setup_inputs(seed: int = 0) -> dict:
    splits = jax.random.split(jax.random.key(seed), 9)
    transmission = jnp.clip(1.0 * jax.random.uniform(splits[0], (N, N), jnp.float32) ** steps_of(splits[0], (N, N), ((0, 4), (1, 4)), -0.2, 0.2), 0.0, 1.0)
    dual_focal = centred(splits[1], (Z, NW, Z), 2.0, 12.0, ((0, 16), (1, 2)), jnp.float32)
    dual_curvature = centred(splits[2], (N, N), 1.0, 6.0, ((0, 4), (1, 4)), jnp.float32)
    pupil_mask = with_ends((jax.random.randint(splits[3], (N, N), 0, 8) < 7).astype(jnp.int32), jax.random.fold_in(splits[3], 1), 0, 1)
    lyot_mask = with_ends((jax.random.randint(splits[4], (N, N), 0, 8) < 7).astype(jnp.int32), jax.random.fold_in(splits[4], 1), 0, 1)
    dark_mask = with_ends((jax.random.randint(splits[5], (Z, NW, Z), 0, 2) < 1).astype(jnp.int32), jax.random.fold_in(splits[5], 1), 0, 1)
    focal_rows = centred(splits[6], (NW, Z, N), N ** -0.5, 0.09375, ((0, 2), (2, 4)), jnp.float32)
    focal_cols = centred(splits[7], (NW, Z, N), N ** -0.5, 0.09375, ((0, 2), (2, 4)), jnp.float32)
    return {"transmission": transmission, "dual_focal": dual_focal, "dual_curvature": dual_curvature, "pupil_mask": pupil_mask, "lyot_mask": lyot_mask, "dark_mask": dark_mask, "focal_rows": focal_rows, "focal_cols": focal_cols}


step_primal = 0.12
step_dual = 0.2
contrast = 0.5
curvature_limit = 0.1


def curvature(field):
    padded = jnp.pad(field, 1)
    beside_all = padded[2:, 1:-1] + padded[:-2, 1:-1] + padded[1:-1, 2:] + padded[1:-1, :-2]
    return 0.25 * beside_all - field


def reference(transmission, dual_focal, dual_curvature, pupil_mask, lyot_mask, dark_mask, focal_rows, focal_cols):
    highest = lax.Precision.HIGHEST
    pupil = pupil_mask.astype(jnp.float32)
    stop = pupil * lyot_mask.astype(jnp.float32)
    dark = dark_mask.astype(jnp.float32)
    primal = transmission
    dual_f = dual_focal * dark
    dual_c = dual_curvature

    def back_one(carry, items):
        rows_table, cols_table, field = items
        carried = jnp.dot(field, cols_table, precision=highest, preferred_element_type=jnp.float32)
        return carry + jnp.dot(rows_table.T, carried, precision=highest, preferred_element_type=jnp.float32), None

    def forward_one(carry, items):
        rows_table, cols_table = items
        left = jnp.dot(rows_table, carry, precision=highest, preferred_element_type=jnp.float32)
        return carry, jnp.dot(left, cols_table.T, precision=highest, preferred_element_type=jnp.float32)

    for iteration in range(ITERS):
        start = jnp.zeros((N, N), jnp.float32)
        backward, _ = lax.scan(back_one, start, (focal_rows, focal_cols, jnp.transpose(dual_f, (1, 0, 2))))
        gradient = -pupil + stop * backward + curvature(dual_c)
        primal_new = jnp.clip(primal - step_primal * gradient, 0.0, 1.0)
        extended = 2.0 * primal_new - primal
        _, fields = lax.scan(forward_one, stop * extended, (focal_rows, focal_cols))
        shifted = dual_f + step_dual * jnp.transpose(fields, (1, 0, 2))
        dual_f = dark * (shifted - step_dual * jnp.clip(shifted / step_dual, -contrast, contrast))
        moved = dual_c + step_dual * curvature(extended)
        dual_c = moved - step_dual * jnp.clip(moved / step_dual, -curvature_limit, curvature_limit)
        primal = primal_new
    return primal, dual_f, dual_c
```

```python
import functools

import jax
import jax.numpy as jnp
from jax import lax
from jax.experimental import pallas as pl
from jax.experimental.pallas import tpu as pltpu
from jax.sharding import PartitionSpec as P

ITERS = 2
step_primal = 0.12
step_dual = 0.2
contrast = 0.5
curvature_limit = 0.1
high = lax.Precision.HIGH
CHUNKS = 2


def around(v, above8, below8, top, bottom, left, right):
    i, last = pl.program_id(0), pl.num_programs(0) - 1
    up = jnp.where(i == 0, top[...], above8[7:8, :])
    down = jnp.where(i == last, bottom[...], below8[0:1, :])
    rows, cols = v.shape
    r = lax.broadcasted_iota(jnp.int32, v.shape, 0)
    c = lax.broadcasted_iota(jnp.int32, v.shape, 1)
    from_up = jnp.where(r == 0, up, pltpu.roll(v, 1, 0))
    from_down = jnp.where(r == rows - 1, down, pltpu.roll(v, rows - 1, 0))
    from_left = jnp.where(c == 0, left[...], pltpu.roll(v, 1, 1))
    from_right = jnp.where(c == cols - 1, right[...], pltpu.roll(v, cols - 1, 1))
    return 0.25 * (from_down + from_up + from_right + from_left) - v


def primal_kernel(mine, other, primal, pupil_m, lyot_m, dual, above, below, top, bottom, left, right, new_ref, ext_ref, mask_ref):
    pupil = pupil_m[...].astype(jnp.float32)
    stop = pupil * lyot_m[...].astype(jnp.float32)
    x = primal[...]
    curv = around(dual[...], above, below, top, bottom, left, right)
    gradient = stop * (mine[...] + other[...]) - pupil + curv
    new = jnp.clip(x - step_primal * gradient, 0.0, 1.0)
    ext = 2.0 * new - x
    new_ref[...] = new
    ext_ref[...] = ext
    mask_ref[...] = stop * ext


def dual_kernel(dual, ext, above, below, top, bottom, left, right, out_ref):
    moved = dual[...] + step_dual * around(ext[...], above, below, top, bottom, left, right)
    out_ref[...] = moved - step_dual * jnp.clip(moved / step_dual, -curvature_limit, curvature_limit)


def specs(rows, cols, block):
    steps, eights = rows // block, block // 8
    whole = pl.BlockSpec((block, cols), lambda i: (i, 0))
    halo = [
        pl.BlockSpec((8, cols), lambda i: (jnp.maximum(i * eights - 1, 0), 0)),
        pl.BlockSpec((8, cols), lambda i: (jnp.minimum((i + 1) * eights, steps * eights - 1), 0)),
        pl.BlockSpec((1, cols), lambda i: (0, 0)),
        pl.BlockSpec((1, cols), lambda i: (0, 0)),
        pl.BlockSpec((block, 1), lambda i: (i, 0)),
        pl.BlockSpec((block, 1), lambda i: (i, 0)),
    ]
    return steps, whole, halo


def primal_step(mine, other, primal, pupil, lyot, dual, edges):
    rows, cols = primal.shape
    steps, whole, halo = specs(rows, cols, 128)
    out = jax.ShapeDtypeStruct((rows, cols), jnp.float32)
    return pl.pallas_call(
        primal_kernel,
        grid=(steps,),
        in_specs=[whole] * 6 + halo,
        out_specs=[whole] * 3,
        out_shape=[out] * 3,
        cost_estimate=pl.CostEstimate(flops=30 * rows * cols, bytes_accessed=36 * rows * cols, transcendentals=0),
    )(mine, other, primal, pupil, lyot, dual, dual, dual, *edges)


def dual_step(dual, ext, edges):
    rows, cols = dual.shape
    steps, whole, halo = specs(rows, cols, 128)
    return pl.pallas_call(
        dual_kernel,
        grid=(steps,),
        in_specs=[whole] * 2 + halo,
        out_specs=whole,
        out_shape=jax.ShapeDtypeStruct((rows, cols), jnp.float32),
        cost_estimate=pl.CostEstimate(flops=20 * rows * cols, bytes_accessed=12 * rows * cols, transcendentals=0),
    )(dual, ext, ext, ext, *edges)


def edges_of(v):
    out = []
    for axis, dim in (("row", 0), ("col", 1)):
        count = lax.axis_size(axis)
        head = lax.slice_in_dim(v, 0, 1, axis=dim)
        tail = lax.slice_in_dim(v, v.shape[dim] - 1, v.shape[dim], axis=dim)
        out.append(lax.ppermute(tail, axis, [(i, i + 1) for i in range(count - 1)]))
        out.append(lax.ppermute(head, axis, [(i + 1, i) for i in range(count - 1)]))
    return out


def gather(part):
    return lax.all_gather(part, ("row", "col"), axis=0, tiled=True)


def scatter(part):
    return lax.psum_scatter(part, ("row", "col"), scatter_dimension=0, tiled=True)


def other_waves(part):
    n = lax.axis_size("wave")
    if n == 1:
        return jnp.zeros_like(part)
    if n == 2:
        return lax.ppermute(part, "wave", [(0, 1), (1, 0)])
    return lax.psum(part, "wave") - part


def per_device(transmission, dual_focal, dual_curvature, pupil_mask, lyot_mask, dark_mask, focal_rows, focal_cols):
    dark = dark_mask.astype(jnp.float32)
    waves = dark.shape[1]
    chunks = CHUNKS if waves % CHUNKS == 0 else 1
    size = waves // chunks
    pieces = [slice(n * size, (n + 1) * size) for n in range(chunks)]
    darks = [dark[:, p] for p in pieces]
    duals = [dual_focal[:, p] * d for p, d in zip(pieces, darks)]
    rows_of = [focal_rows[p] for p in pieces]
    cols_of = [focal_cols[p] for p in pieces]
    primal, dual_c = transmission, dual_curvature
    fulls = [gather(d) for d in duals]
    for iteration in range(ITERS):
        dual_edges = edges_of(dual_c)
        carried = [jnp.einsum("kwz,wzc->kwc", f, c, precision=high) for f, c in zip(fulls, cols_of)]
        backward = functools.reduce(
            jnp.add, [jnp.einsum("wkr,kwc->rc", r, c, precision=high) for r, c in zip(rows_of, carried)]
        )
        other = other_waves(backward)
        primal, extended, masked = primal_step(backward, other, primal, pupil_mask, lyot_mask, dual_c, dual_edges)
        new_duals = []
        fulls = []
        for r, c, d, k in zip(rows_of, cols_of, duals, darks):
            left = jnp.einsum("wkr,rc->kwc", r, masked, precision=high)
            fields = scatter(jnp.einsum("kwc,wzc->kwz", left, c, precision=high))
            shifted = d + step_dual * fields
            new = k * (shifted - step_dual * jnp.clip(shifted / step_dual, -contrast, contrast))
            new_duals.append(new)
            if iteration < ITERS - 1:
                fulls.append(gather(new))
        duals = new_duals
        dual_c = dual_step(dual_c, extended, edges_of(extended))
    return (primal, jnp.concatenate(duals, axis=1), dual_c)


def solution(mesh):
    return jax.shard_map(
        per_device,
        mesh=mesh,
        in_specs=(
            P("row", "col"),
            P(("row", "col"), "wave", None),
            P("row", "col"),
            P("row", "col"),
            P("row", "col"),
            P(("row", "col"), "wave", None),
            P("wave", None, "row"),
            P("wave", None, "col"),
        ),
        out_specs=(P("row", "col"), P(("row", "col"), "wave", None), P("row", "col")),
        check_vma=False,
    )
```

```python
import functools

import jax
import jax.numpy as jnp
from jax import lax
from jax.experimental import pallas as pl
from jax.experimental.pallas import tpu as pltpu
from jax.sharding import PartitionSpec as P

ITERS = 2
step_primal = 0.12
step_dual = 0.2
contrast = 0.5
curvature_limit = 0.1
high = lax.Precision.HIGH
CHUNKS = 1


def around(v, above8, below8, top, bottom, left, right):
    i, last = pl.program_id(0), pl.num_programs(0) - 1
    up = jnp.where(i == 0, top[...], above8[7:8, :])
    down = jnp.where(i == last, bottom[...], below8[0:1, :])
    rows, cols = v.shape
    r = lax.broadcasted_iota(jnp.int32, v.shape, 0)
    c = lax.broadcasted_iota(jnp.int32, v.shape, 1)
    from_up = jnp.where(r == 0, up, pltpu.roll(v, 1, 0))
    from_down = jnp.where(r == rows - 1, down, pltpu.roll(v, rows - 1, 0))
    from_left = jnp.where(c == 0, left[...], pltpu.roll(v, 1, 1))
    from_right = jnp.where(c == cols - 1, right[...], pltpu.roll(v, cols - 1, 1))
    return 0.25 * (from_down + from_up + from_right + from_left) - v


def primal_kernel(mine, other, primal, pupil_m, lyot_m, dual, above, below, top, bottom, left, right, new_ref, ext_ref, mask_ref):
    pupil = pupil_m[...].astype(jnp.float32)
    stop = pupil * lyot_m[...].astype(jnp.float32)
    x = primal[...]
    curv = around(dual[...], above, below, top, bottom, left, right)
    gradient = stop * (mine[...] + other[...]) - pupil + curv
    new = jnp.clip(x - step_primal * gradient, 0.0, 1.0)
    ext = 2.0 * new - x
    new_ref[...] = new
    ext_ref[...] = ext
    mask_ref[...] = stop * ext


def dual_kernel(dual, ext, above, below, top, bottom, left, right, out_ref):
    moved = dual[...] + step_dual * around(ext[...], above, below, top, bottom, left, right)
    out_ref[...] = moved - step_dual * jnp.clip(moved / step_dual, -curvature_limit, curvature_limit)


def specs(rows, cols, block):
    steps, eights = rows // block, block // 8
    whole = pl.BlockSpec((block, cols), lambda i: (i, 0))
    halo = [
        pl.BlockSpec((8, cols), lambda i: (jnp.maximum(i * eights - 1, 0), 0)),
        pl.BlockSpec((8, cols), lambda i: (jnp.minimum((i + 1) * eights, steps * eights - 1), 0)),
        pl.BlockSpec((1, cols), lambda i: (0, 0)),
        pl.BlockSpec((1, cols), lambda i: (0, 0)),
        pl.BlockSpec((block, 1), lambda i: (i, 0)),
        pl.BlockSpec((block, 1), lambda i: (i, 0)),
    ]
    return steps, whole, halo


def primal_step(mine, other, primal, pupil, lyot, dual, edges):
    rows, cols = primal.shape
    steps, whole, halo = specs(rows, cols, 128)
    out = jax.ShapeDtypeStruct((rows, cols), jnp.float32)
    return pl.pallas_call(
        primal_kernel,
        grid=(steps,),
        in_specs=[whole] * 6 + halo,
        out_specs=[whole] * 3,
        out_shape=[out] * 3,
        cost_estimate=pl.CostEstimate(flops=30 * rows * cols, bytes_accessed=36 * rows * cols, transcendentals=0),
    )(mine, other, primal, pupil, lyot, dual, dual, dual, *edges)


def dual_step(dual, ext, edges):
    rows, cols = dual.shape
    steps, whole, halo = specs(rows, cols, 128)
    return pl.pallas_call(
        dual_kernel,
        grid=(steps,),
        in_specs=[whole] * 2 + halo,
        out_specs=whole,
        out_shape=jax.ShapeDtypeStruct((rows, cols), jnp.float32),
        cost_estimate=pl.CostEstimate(flops=20 * rows * cols, bytes_accessed=12 * rows * cols, transcendentals=0),
    )(dual, ext, ext, ext, *edges)


def edges_of(v):
    out = []
    for axis, dim in (("row", 0), ("col", 1)):
        count = lax.axis_size(axis)
        head = lax.slice_in_dim(v, 0, 1, axis=dim)
        tail = lax.slice_in_dim(v, v.shape[dim] - 1, v.shape[dim], axis=dim)
        out.append(lax.ppermute(tail, axis, [(i, i + 1) for i in range(count - 1)]))
        out.append(lax.ppermute(head, axis, [(i + 1, i) for i in range(count - 1)]))
    return out


def gather(part):
    return lax.all_gather(part, ("row", "col"), axis=0, tiled=True)


def scatter(part):
    return lax.psum_scatter(part, ("row", "col"), scatter_dimension=0, tiled=True)


def other_waves(part):
    n = lax.axis_size("wave")
    if n == 1:
        return jnp.zeros_like(part)
    if n == 2:
        return lax.ppermute(part, "wave", [(0, 1), (1, 0)])
    return lax.psum(part, "wave") - part


def per_device(transmission, dual_focal, dual_curvature, pupil_mask, lyot_mask, dark_mask, focal_rows, focal_cols):
    dark = dark_mask.astype(jnp.float32)
    waves = dark.shape[1]
    chunks = CHUNKS if waves % CHUNKS == 0 else 1
    size = waves // chunks
    pieces = [slice(n * size, (n + 1) * size) for n in range(chunks)]
    darks = [dark[:, p] for p in pieces]
    duals = [dual_focal[:, p] * d for p, d in zip(pieces, darks)]
    rows_of = [focal_rows[p] for p in pieces]
    cols_of = [focal_cols[p] for p in pieces]
    primal, dual_c = transmission, dual_curvature
    fulls = [gather(d) for d in duals]
    for iteration in range(ITERS):
        if iteration == 0:
            dual_edges = edges_of(dual_c)
            fulls, dual_edges = lax.optimization_barrier((fulls, dual_edges))
        carried = [jnp.einsum("kwz,wzc->kwc", f, c, precision=high) for f, c in zip(fulls, cols_of)]
        backward = functools.reduce(
            jnp.add, [jnp.einsum("wkr,kwc->rc", r, c, precision=high) for r, c in zip(rows_of, carried)]
        )
        other = other_waves(backward)
        primal, extended, masked = primal_step(backward, other, primal, pupil_mask, lyot_mask, dual_c, dual_edges)
        new_duals = []
        fulls = []
        summed = []
        for r, c in zip(rows_of, cols_of):
            left = jnp.einsum("wkr,rc->kwc", r, masked, precision=high)
            summed.append(scatter(jnp.einsum("kwc,wzc->kwz", left, c, precision=high)))
        dual_c = dual_step(dual_c, extended, edges_of(extended))
        if iteration < ITERS - 1:
            dual_edges = edges_of(dual_c)
            summed, dual_c, dual_edges = lax.optimization_barrier((summed, dual_c, dual_edges))
        for fields, d, k in zip(summed, duals, darks):
            shifted = d + step_dual * fields
            new = k * (shifted - step_dual * jnp.clip(shifted / step_dual, -contrast, contrast))
            new_duals.append(new)
            if iteration < ITERS - 1:
                fulls.append(gather(new))
        duals = new_duals
    return (primal, jnp.concatenate(duals, axis=1), dual_c)


def solution(mesh):
    return jax.shard_map(
        per_device,
        mesh=mesh,
        in_specs=(
            P("row", "col"),
            P(("row", "col"), "wave", None),
            P("row", "col"),
            P("row", "col"),
            P("row", "col"),
            P(("row", "col"), "wave", None),
            P("wave", None, "row"),
            P("wave", None, "col"),
        ),
        out_specs=(P("row", "col"), P(("row", "col"), "wave", None), P("row", "col")),
        check_vma=False,
    )
```

```python
import functools

import jax
import jax.numpy as jnp
from jax import lax
from jax.experimental import pallas as pl
from jax.experimental.pallas import tpu as pltpu
from jax.sharding import PartitionSpec as P

ITERS = 2
step_primal = 0.12
step_dual = 0.2
contrast = 0.5
curvature_limit = 0.1
high = lax.Precision.HIGH
CHUNKS = 1
MESH = pl.DeviceIdType.MESH


def around(v, above8, below8, top, bottom, left, right):
    i, last = pl.program_id(0), pl.num_programs(0) - 1
    up = jnp.where(i == 0, top[...], above8[7:8, :])
    down = jnp.where(i == last, bottom[...], below8[0:1, :])
    rows, cols = v.shape
    r = lax.broadcasted_iota(jnp.int32, v.shape, 0)
    c = lax.broadcasted_iota(jnp.int32, v.shape, 1)
    from_up = jnp.where(r == 0, up, pltpu.roll(v, 1, 0))
    from_down = jnp.where(r == rows - 1, down, pltpu.roll(v, rows - 1, 0))
    from_left = jnp.where(c == 0, left[...], pltpu.roll(v, 1, 1))
    from_right = jnp.where(c == cols - 1, right[...], pltpu.roll(v, cols - 1, 1))
    return 0.25 * (from_down + from_up + from_right + from_left) - v


def primal_kernel(mine, other, primal, pupil_m, lyot_m, dual, above, below, top, bottom, left, right, new_ref, ext_ref, mask_ref):
    pupil = pupil_m[...].astype(jnp.float32)
    stop = pupil * lyot_m[...].astype(jnp.float32)
    x = primal[...]
    curv = around(dual[...], above, below, top, bottom, left, right)
    gradient = stop * (mine[...] + other[...]) - pupil + curv
    new = jnp.clip(x - step_primal * gradient, 0.0, 1.0)
    ext = 2.0 * new - x
    new_ref[...] = new
    ext_ref[...] = ext
    mask_ref[...] = stop * ext


def dual_kernel(dual, ext, above, below, top, bottom, left, right, out_ref):
    moved = dual[...] + step_dual * around(ext[...], above, below, top, bottom, left, right)
    out_ref[...] = moved - step_dual * jnp.clip(moved / step_dual, -curvature_limit, curvature_limit)


def specs(rows, cols, block):
    steps, eights = rows // block, block // 8
    whole = pl.BlockSpec((block, cols), lambda i: (i, 0))
    halo = [
        pl.BlockSpec((8, cols), lambda i: (jnp.maximum(i * eights - 1, 0), 0)),
        pl.BlockSpec((8, cols), lambda i: (jnp.minimum((i + 1) * eights, steps * eights - 1), 0)),
        pl.BlockSpec((1, cols), lambda i: (0, 0)),
        pl.BlockSpec((1, cols), lambda i: (0, 0)),
        pl.BlockSpec((block, 1), lambda i: (i, 0)),
        pl.BlockSpec((block, 1), lambda i: (i, 0)),
    ]
    return steps, whole, halo


def primal_step(mine, other, primal, pupil, lyot, dual, edges):
    rows, cols = primal.shape
    steps, whole, halo = specs(rows, cols, 128)
    out = jax.ShapeDtypeStruct((rows, cols), jnp.float32)
    return pl.pallas_call(
        primal_kernel,
        grid=(steps,),
        in_specs=[whole] * 6 + halo,
        out_specs=[whole] * 3,
        out_shape=[out] * 3,
        cost_estimate=pl.CostEstimate(flops=30 * rows * cols, bytes_accessed=36 * rows * cols, transcendentals=0),
    )(mine, other, primal, pupil, lyot, dual, dual, dual, *edges)


def dual_step(dual, ext, edges):
    rows, cols = dual.shape
    steps, whole, halo = specs(rows, cols, 128)
    return pl.pallas_call(
        dual_kernel,
        grid=(steps,),
        in_specs=[whole] * 2 + halo,
        out_specs=whole,
        out_shape=jax.ShapeDtypeStruct((rows, cols), jnp.float32),
        cost_estimate=pl.CostEstimate(flops=20 * rows * cols, bytes_accessed=12 * rows * cols, transcendentals=0),
    )(dual, ext, ext, ext, *edges)


def edges_of(v):
    out = []
    for axis, dim in (("row", 0), ("col", 1)):
        count = lax.axis_size(axis)
        head = lax.slice_in_dim(v, 0, 1, axis=dim)
        tail = lax.slice_in_dim(v, v.shape[dim] - 1, v.shape[dim], axis=dim)
        out.append(lax.ppermute(tail, axis, [(i, i + 1) for i in range(count - 1)]))
        out.append(lax.ppermute(head, axis, [(i + 1, i) for i in range(count - 1)]))
    return out


def greet():
    r, c, nr, nc = lax.axis_index("row"), lax.axis_index("col"), lax.axis_size("row"), lax.axis_size("col")
    barrier = pltpu.get_barrier_semaphore()
    for d in range(1, nr):
        pl.semaphore_signal(barrier, inc=1, device_id={"row": lax.rem(r + d, nr)}, device_id_type=MESH)
    for e in range(1, nc):
        pl.semaphore_signal(barrier, inc=1, device_id={"col": lax.rem(c + e, nc)}, device_id_type=MESH)
    pl.semaphore_wait(barrier, nr + nc - 2)
    return r, c, nr, nc


def gather_kernel(x_ref, out_ref, send_r, recv_r, send_c, recv_c):
    r, c, nr, nc = greet()
    mine = r * nc + c
    sent = []
    for d in range(1, nr):
        copy = pltpu.make_async_remote_copy(
            src_ref=x_ref, dst_ref=out_ref.at[mine], send_sem=send_r.at[d], recv_sem=recv_r.at[d],
            device_id={"row": lax.rem(r + d, nr)}, device_id_type=MESH)
        copy.start()
        sent.append(copy)
    along = list(sent)
    across = []
    for d in range(nr):
        slot = lax.rem(r + nr - d, nr) * nc + c
        if d > 0:
            along[d - 1].wait_recv()
        for e in range(1, nc):
            copy = pltpu.make_async_remote_copy(
                src_ref=x_ref if d == 0 else out_ref.at[slot], dst_ref=out_ref.at[slot],
                send_sem=send_c.at[d * nc + e], recv_sem=recv_c.at[d * nc + e],
                device_id={"col": lax.rem(c + e, nc)}, device_id_type=MESH)
            copy.start()
            across.append(copy)
    out_ref[mine] = x_ref[...]
    for copy in across:
        copy.wait_recv()
    for copy in along + across:
        copy.wait_send()


def scatter_kernel(x_ref, out_ref, got_c, part, got_r, send_r, recv_r, send_c, recv_c):
    r, c, nr, nc = greet()
    across, along = {}, []
    for d in list(range(1, nr)) + [0]:
        for e in range(1, nc):
            slot = lax.rem(r + d, nr) * nc + lax.rem(c + e, nc)
            copy = pltpu.make_async_remote_copy(
                src_ref=x_ref.at[slot], dst_ref=got_c.at[d * nc + e],
                send_sem=send_c.at[d * nc + e], recv_sem=recv_c.at[d * nc + e],
                device_id={"col": lax.rem(c + e, nc)}, device_id_type=MESH)
            copy.start()
            across[d, e] = copy
    for d in list(range(1, nr)) + [0]:
        total = x_ref[lax.rem(r + d, nr) * nc + c]
        for e in range(1, nc):
            across[d, e].wait_recv()
            total = total + got_c[d * nc + e]
        part[d] = total
        if d > 0:
            copy = pltpu.make_async_remote_copy(
                src_ref=part.at[d], dst_ref=got_r.at[d], send_sem=send_r.at[d], recv_sem=recv_r.at[d],
                device_id={"row": lax.rem(r + d, nr)}, device_id_type=MESH)
            copy.start()
            along.append(copy)
    total = part[0]
    for d in range(1, nr):
        along[d - 1].wait_recv()
        total = total + got_r[d]
    out_ref[...] = total
    for copy in list(across.values()) + along:
        copy.wait_send()


def sems(nr, nc):
    dma = pltpu.SemaphoreType.DMA
    return [dma((nr,)), dma((nr,)), dma((nr * nc,)), dma((nr * nc,))]


def gather(part):
    nr, nc = lax.axis_size("row"), lax.axis_size("col")
    k, w, z = part.shape
    out = pl.pallas_call(
        gather_kernel,
        in_specs=[pl.BlockSpec(memory_space=pltpu.VMEM)],
        out_specs=pl.BlockSpec(memory_space=pltpu.VMEM),
        out_shape=jax.ShapeDtypeStruct((nr * nc, k * w, z), jnp.float32),
        scratch_shapes=sems(nr, nc),
        compiler_params=pltpu.CompilerParams(collective_id=0, has_side_effects=True),
    )(part.reshape(k * w, z))
    return out.reshape(nr * nc * k, w, z)


def scatter(part):
    nr, nc = lax.axis_size("row"), lax.axis_size("col")
    k, w, z = part.shape
    size = (k // (nr * nc)) * w
    block = lambda n: pltpu.VMEM((n, size, z), jnp.float32)
    out = pl.pallas_call(
        scatter_kernel,
        in_specs=[pl.BlockSpec(memory_space=pltpu.VMEM)],
        out_specs=pl.BlockSpec(memory_space=pltpu.VMEM),
        out_shape=jax.ShapeDtypeStruct((size, z), jnp.float32),
        scratch_shapes=[block(nr * nc), block(nr), block(nr)] + sems(nr, nc),
        compiler_params=pltpu.CompilerParams(collective_id=1, has_side_effects=True),
    )(part.reshape(nr * nc, size, z))
    return out.reshape(k // (nr * nc), w, z)


def other_waves(part):
    n = lax.axis_size("wave")
    if n == 1:
        return jnp.zeros_like(part)
    if n == 2:
        return lax.ppermute(part, "wave", [(0, 1), (1, 0)])
    return lax.psum(part, "wave") - part


def per_device(transmission, dual_focal, dual_curvature, pupil_mask, lyot_mask, dark_mask, focal_rows, focal_cols):
    dark = dark_mask.astype(jnp.float32)
    waves = dark.shape[1]
    chunks = CHUNKS if waves % CHUNKS == 0 else 1
    size = waves // chunks
    pieces = [slice(n * size, (n + 1) * size) for n in range(chunks)]
    darks = [dark[:, p] for p in pieces]
    duals = [dual_focal[:, p] * d for p, d in zip(pieces, darks)]
    rows_of = [focal_rows[p] for p in pieces]
    cols_of = [focal_cols[p] for p in pieces]
    primal, dual_c = transmission, dual_curvature
    fulls = [gather(d) for d in duals]
    for iteration in range(ITERS):
        if iteration == 0:
            dual_edges = edges_of(dual_c)
            fulls, dual_edges = lax.optimization_barrier((fulls, dual_edges))
        carried = [jnp.einsum("kwz,wzc->kwc", f, c, precision=high) for f, c in zip(fulls, cols_of)]
        backward = functools.reduce(
            jnp.add, [jnp.einsum("wkr,kwc->rc", r, c, precision=high) for r, c in zip(rows_of, carried)]
        )
        other = other_waves(backward)
        primal, extended, masked = primal_step(backward, other, primal, pupil_mask, lyot_mask, dual_c, dual_edges)
        new_duals = []
        fulls = []
        summed = []
        for r, c in zip(rows_of, cols_of):
            left = jnp.einsum("wkr,rc->kwc", r, masked, precision=high)
            summed.append(scatter(jnp.einsum("kwc,wzc->kwz", left, c, precision=high)))
        dual_c = dual_step(dual_c, extended, edges_of(extended))
        if iteration < ITERS - 1:
            dual_edges = edges_of(dual_c)
            summed, dual_c, dual_edges = lax.optimization_barrier((summed, dual_c, dual_edges))
        for fields, d, k in zip(summed, duals, darks):
            shifted = d + step_dual * fields
            new = k * (shifted - step_dual * jnp.clip(shifted / step_dual, -contrast, contrast))
            new_duals.append(new)
            if iteration < ITERS - 1:
                fulls.append(gather(new))
        duals = new_duals
    return (primal, jnp.concatenate(duals, axis=1), dual_c)


def solution(mesh):
    return jax.shard_map(
        per_device,
        mesh=mesh,
        in_specs=(
            P("row", "col"),
            P(("row", "col"), "wave", None),
            P("row", "col"),
            P("row", "col"),
            P("row", "col"),
            P(("row", "col"), "wave", None),
            P("wave", None, "row"),
            P("wave", None, "col"),
        ),
        out_specs=(P("row", "col"), P(("row", "col"), "wave", None), P("row", "col")),
        check_vma=False,
    )
```
